256 devices in a mesh: mem: 4 (over y_hi, core), strip: 64 (over x, y_lo, z).
Axes of the slice: x: 4, y: 4 (y_hi: 2, y_lo: 2; y = y_hi * 2 + y_lo), z: 8, core: 2. Of those that a mesh axis runs over, the one named last changes fastest.
Arguments:
- gradient: float32 [8, 2048, 1024], P('mem', 'strip'), may hold values from -6 to 6
- perturbations: bfloat16 [64, 8, 2048, 1024], P('mem', None, 'strip'), may hold values from -6 to 6
- counts: int32 [2048, 1024], P('strip'), may hold values from 1 to 4, as said below
Outputs:
- increment: float32 [8, 2048, 1024], P('mem', 'strip')
The draws below stay inside these ranges and needn't reach their ends.
Inputs may be any that keep to these rules, and one draw needn't show every extreme that they name: `counts`: counts are drawn band by band of 32 rows along the first dimension, each band under a cap of its own; some cell reaches 4.
All inputs are finite; a program needn't handle non-finite values.
Results may differ from the reference program's by a relative error of at most 0.0003.
Values sent between devices are 32-bit elements; how exact they have to be, the bound alone decides.
A program may use at most 64 MiB of HBM per device.

```python
import math
import jax
import jax.numpy as jnp
from jax import lax

SLOTS = 2
VARS = 4
FIELDS = 8
SWEEPS = 4
MEMB_DEV = 16
MEMBERS = 64
CX = 32
NY = 1024
NX = 2048
N_MEM = 4


def draw_counts(key, part):
    key_caps = jax.random.fold_in(key, 11)
    key_cells = jax.random.fold_in(key, 12)
    band_count = NX // CX
    band_caps = jax.random.randint(key_caps, (band_count,), 1, SWEEPS + 1)
    band_caps = band_caps.at[0].set(SWEEPS)
    row_caps = jnp.repeat(band_caps, CX)
    raw_cells = jax.random.randint(key_cells, (NX, NY), 0, 1 << 20)
    result = 1 + raw_cells % row_caps[:, None]
    result = result.at[0, 0].set(SWEEPS)
    return result.astype(jnp.int32)


def levels(stream_key, shape, cuts, least, high):
    gain, own = 1.0, jax.random.fold_in(stream_key, 6)
    for axis_at, blocks in cuts:
        steps = jnp.exp(jax.random.uniform(jax.random.fold_in(own, axis_at), (blocks,), jnp.float32, least / len(cuts), high / len(cuts)))
        gain = gain * jnp.repeat(steps, shape[axis_at] // blocks).reshape([-1 if axis == axis_at else 1 for axis in range(len(shape))])
    return gain


def scatter_about(own_key, extent, spread, reach, split=(), kind=jnp.bfloat16):
    factor_of = levels(own_key, extent, split, -0.22, 0.18) if split else 1.0
    entries = jax.random.normal(own_key, extent, jnp.float32) * spread * factor_of
    return jnp.minimum(jnp.maximum(entries, -reach), reach).astype(kind)


def setup_inputs(seed: int = 0) -> dict:
    splits = jax.random.split(jax.random.key(seed), 4)
    gradient = scatter_about(splits[0], (FIELDS, NX, NY), 1.0, 6.0, ((0, 4), (1, 64)), jnp.float32)
    perturbations = scatter_about(splits[1], (MEMBERS, FIELDS, NX, NY), 1.0, 6.0, ((0, 4), (2, 64)))
    counts = draw_counts(jax.random.fold_in(splits[3], 71), 0)
    return {"gradient": gradient, "perturbations": perturbations, "counts": counts}


COEFF_X = 0.35
COEFF_Y = 0.12

def sweep_once(state_field, active):
    widths = ((0, 0), (0, 0), (1, 1), (1, 1))
    padded = jnp.pad(state_field, widths)
    along_x = padded[:, :, 2:, 1:-1] + padded[:, :, :-2, 1:-1] - 2.0 * state_field
    along_y = padded[:, :, 1:-1, 2:] + padded[:, :, 1:-1, :-2] - 2.0 * state_field
    return state_field + active * (COEFF_X * along_x + COEFF_Y * along_y)

def reference(gradient, perturbations, counts):
    grad_slots = gradient.reshape(SLOTS, VARS, NX, NY)
    grouped = perturbations.reshape(N_MEM, MEMB_DEV, FIELDS, NX, NY)

    def accumulate(running, member_block):
        block_values = member_block.astype(jnp.float32).reshape(MEMB_DEV, SLOTS, VARS, NX, NY)
        state_field = lax.optimization_barrier(jnp.sum(block_values * grad_slots[None], axis=2))
        for sweep_index in range(SWEEPS):
            active = (counts > sweep_index).astype(jnp.float32)
            state_field = sweep_once(state_field, active)
        member_term = lax.optimization_barrier(jnp.sum(block_values * state_field[:, :, None], axis=0))
        return (running + member_term.reshape(FIELDS, NX, NY), None)
    running, unused = lax.scan(accumulate, jnp.zeros((FIELDS, NX, NY), jnp.float32), grouped)
    return running * (1.0 / math.sqrt(MEMBERS * FIELDS))
```

```python
import math

import jax
import jax.numpy as jnp
from jax import lax
from jax.experimental import pallas as pl
from jax.experimental.pallas import tpu as pltpu
from jax.sharding import PartitionSpec as P

MESH = pl.DeviceIdType.MESH
SLOTS, VARS, FIELDS, SWEEPS = 2, 4, 8, 4
CX, NY, K = 32, 1024, 16
LANES = 128
CB = NY // LANES
HALO = SWEEPS
UNROLL = 2
KX, KY = 0.35, 0.12
ALPHA = KY / KX
GAMMA = (1.0 - 2.0 * KX - 2.0 * KY) / KX
BETA = 2.0 + 2.0 * ALPHA
PITCH = 9
PIECES = ((0, 8), (24, 8), (8, 16))


def remote(src, dst, send, recv, device):
    return pltpu.make_async_remote_copy(
        src_ref=src, dst_ref=dst, send_sem=send, recv_sem=recv, device_id=device, device_id_type=MESH
    )


def lanes_of(cb):
    return pl.ds(pl.multiple_of(cb * LANES, LANES), LANES)


def kernel(
    norm, strips,
    grad, pert, counts, own_ref, other_ref,
    pv, gv, cv, ct, cn, u, near, sent, edge, coef, inc, part, csum, osum,
    pert_sem, load_sem, gsend, grecv, csend, crecv, hsend, hrecv, psend, precv, rsend, rrecv, out_sem,
):
    m, s = lax.axis_index("mem"), lax.axis_index("strip")
    chip, core = lax.div(m, 2), lax.rem(m, 2)
    m1, m2 = m + 1 - 2 * core, lax.rem(m + 2, 4)
    m3 = m2 + 1 - 2 * core
    mine, theirs = chip, 1 - chip
    has_up, has_down = s > 0, s < strips - 1
    slots = (mine, theirs)

    loads = []
    for i, (first, size) in enumerate(PIECES):
        for j, sl in enumerate(slots):
            fields, rows = pl.ds(sl * VARS, VARS), pl.ds(first, size)
            loads.append(pltpu.make_async_copy(
                pert.at[:, fields, rows, :], pv.at[:, fields, rows, :], pert_sem.at[j, i]))
    load_g = pltpu.make_async_copy(grad, gv.at[m], load_sem.at[0])
    load_c = pltpu.make_async_copy(counts, cv, load_sem.at[1])
    load_g.start()
    load_c.start()
    for copy in loads:
        copy.start()

    barrier = pltpu.get_barrier_semaphore()
    for device in ((m1, s), (m2, s)):
        pl.semaphore_signal(barrier, inc=1, device_id=device, device_id_type=MESH)

    @pl.when(has_up)
    def _():
        pl.semaphore_signal(barrier, inc=1, device_id=(m, s - 1), device_id_type=MESH)

    @pl.when(has_down)
    def _():
        pl.semaphore_signal(barrier, inc=1, device_id=(m, s + 1), device_id_type=MESH)

    pl.semaphore_wait(barrier, 2 + has_up.astype(jnp.int32) + has_down.astype(jnp.int32))

    to_core, to_chip, onward = [], [], []
    for i, (first, size) in enumerate(PIECES):
        rows = pl.ds(first, size)
        to_core.append(remote(grad.at[:, rows, :], gv.at[m, :, rows, :], gsend.at[0, i], grecv.at[0, i], (m1, s)))
        to_chip.append(remote(grad.at[:, rows, :], gv.at[m, :, rows, :], gsend.at[1, i], grecv.at[1, i], (m2, s)))
        onward.append(remote(
            gv.at[m2, :, rows, :], gv.at[m2, :, rows, :], gsend.at[2, i], grecv.at[2, i], (m1, s)))
    c_up = remote(counts.at[pl.ds(0, 8), :], cn, csend.at[0], crecv.at[0], (m, s - 1))
    c_down = remote(counts.at[pl.ds(24, 8), :], ct, csend.at[1], crecv.at[1], (m, s + 1))

    def halos(sl):
        up = remote(sent.at[sl, 0], near.at[sl, 1],
                    hsend.at[sl, 0], hrecv.at[sl, 0], (m, s - 1))
        down = remote(sent.at[sl, 1], near.at[sl, 0],
                      hsend.at[sl, 1], hrecv.at[sl, 1], (m, s + 1))
        return up, down

    def start_both(up, down):
        @pl.when(has_up)
        def _():
            up.start()

        @pl.when(has_down)
        def _():
            down.start()

    def wait_recv_both(up, down):
        @pl.when(has_down)
        def _():
            up.wait_recv()

        @pl.when(has_up)
        def _():
            down.wait_recv()

    def wait_send_both(up, down):
        @pl.when(has_up)
        def _():
            up.wait_send()

        @pl.when(has_down)
        def _():
            down.wait_send()

    start_both(c_up, c_down)
    for i in range(2):
        to_chip[i].start()
        to_core[i].start()

    def project(sl, pieces):
        def column(cb, carry):
            lanes = lanes_of(cb)
            for first, size in pieces:
                rows = pl.ds(first, size)
                g = [gv[2 * sl + v // 2, v % 2, rows, lanes] for v in range(VARS)]
                for k in range(K):
                    total = pv[k, sl * VARS, rows, lanes].astype(jnp.float32) * g[0]
                    for v in range(1, VARS):
                        total = total + pv[k, sl * VARS + v, rows, lanes].astype(jnp.float32) * g[v]
                    for i in range(0, size, 8):
                        u[sl, k // 8, cb, pl.ds((first + i) * PITCH + k % 8, 8, stride=PITCH), :] = total[i : i + 8]
            for side, x0 in ((0, 0), (1, CX - HALO)):
                if any(first <= x0 < first + size for first, size in pieces):
                    for i in range(HALO):
                        for h in range(2):
                            sent[sl, side, h, cb, i] = u[sl, h, cb, pl.ds((x0 + i) * PITCH, 8), :]
            return carry

        lax.fori_loop(0, CB, column, 0, unroll=UNROLL)

    def zero_outside(sl):
        @pl.when(jnp.logical_not(has_up))
        def _():
            near[sl, 0] = jnp.zeros(near.shape[2:], jnp.float32)

        @pl.when(jnp.logical_not(has_down))
        def _():
            near[sl, 1] = jnp.zeros(near.shape[2:], jnp.float32)

    lane = lax.broadcasted_iota(jnp.int32, (8, LANES), 1)
    at_first, at_last = lane == 0, lane == LANES - 1
    zero = jnp.zeros((8, LANES), jnp.float32)
    on_grid = [jnp.where(has, jnp.ones((8, LANES), jnp.float32), 0.0) for has in (has_up, has_down)]

    def row_of(sl, x, h):
        if x < 0:
            return [near[sl, 0, h, cb, HALO + x] for cb in range(CB)]
        if x >= CX:
            return [near[sl, 1, h, cb, x - CX] for cb in range(CB)]
        return [u[sl, h, cb, pl.ds(x * PITCH, 8), :] for cb in range(CB)]

    def put_row(sl, x, h, values):
        for cb in range(CB):
            if x < 0:
                near[sl, 0, h, cb, HALO + x] = values[cb]
            elif x >= CX:
                near[sl, 1, h, cb, x - CX] = values[cb]
            else:
                u[sl, h, cb, pl.ds(x * PITCH, 8), :] = values[cb]

    def advanced(before, centre, after, t, x):
        right = [pltpu.roll(c, 1, 1) for c in centre]
        left = [pltpu.roll(c, LANES - 1, 1) for c in centre]
        out = []
        for cb in range(CB):
            low = jnp.where(at_first, right[cb - 1] if cb > 0 else zero, right[cb])
            high = jnp.where(at_last, left[cb + 1] if cb < CB - 1 else zero, left[cb])
            total = (before[cb] + after[cb]) + ALPHA * (low + high)
            if t == 0:
                total = total + GAMMA * centre[cb]
                out.append(total if 0 <= x < CX else on_grid[x >= CX] * total)
            else:
                out.append(centre[cb] + coef[t - 1, cb, HALO + x] * (total - BETA * centre[cb]))
        return out

    def inner_sweeps(sl, halves):
        def half(h, carry):
            for t in range(SWEEPS):
                first, last = t + 1, CX - 2 - t
                before, centre = row_of(sl, first - 1, h), row_of(sl, first, h)
                for cb in range(CB):
                    edge[sl, 0, t, h, cb] = centre[cb]
                for x in range(first, last + 1):
                    after = row_of(sl, x + 1, h)
                    if x == last:
                        for cb in range(CB):
                            edge[sl, 1, t, h, cb] = centre[cb]
                    put_row(sl, x, h, advanced(before, centre, after, t, x))
                    before, centre = centre, after
            return carry

        lax.fori_loop(*halves, half, 0)

    def outer_sweeps(sl):
        def half(h, carry):
            for t in range(SWEEPS):
                before, centre = row_of(sl, t - HALO, h), row_of(sl, t - HALO + 1, h)
                for x in range(t - HALO + 1, t + 1):
                    after = [edge[sl, 0, t, h, cb] for cb in range(CB)] if x == t else row_of(sl, x + 1, h)
                    put_row(sl, x, h, advanced(before, centre, after, t, x))
                    before, centre = centre, after
                before, centre = [edge[sl, 1, t, h, cb] for cb in range(CB)], row_of(sl, CX - 1 - t, h)
                for x in range(CX - 1 - t, CX + HALO - 1 - t):
                    after = row_of(sl, x + 1, h)
                    put_row(sl, x, h, advanced(before, centre, after, t, x))
                    before, centre = centre, after
            return carry

        lax.fori_loop(0, 2, half, 0)

    def increments(sl, pieces):
        def column(cb, carry):
            lanes = lanes_of(cb)
            for first, size in pieces:
                for x in range(first, first + size, 8):
                    rows = pl.ds(x, 8)
                    total = [None] * VARS
                    for k in range(K):
                        smooth = u[sl, k // 8, cb, pl.ds(x * PITCH + k % 8, 8, stride=PITCH), :]
                        for v in range(VARS):
                            term = pv[k, sl * VARS + v, rows, lanes].astype(jnp.float32) * smooth
                            total[v] = term if k == 0 else total[v] + term
                    for v in range(VARS):
                        inc[sl, v // 2, v % 2, rows, lanes] = total[v] * (norm * KX)
            return carry

        lax.fori_loop(0, CB, column, 0, unroll=UNROLL)

    def to_partner(sl, i):
        rows = pl.ds(*PIECES[i])
        return remote(inc.at[sl, 1 - core, :, rows, :], part.at[sl, :, rows, :],
                      psend.at[sl, i], precv.at[sl, i], (m1, s))

    def to_owner(i):
        rows = pl.ds(*PIECES[i])
        return remote(csum.at[:, rows, :], other_ref.at[:, rows, :], rsend.at[i], rrecv.at[i], (m2, s))

    def out_copy(i):
        rows = pl.ds(*PIECES[i])
        return pltpu.make_async_copy(osum.at[:, rows, :], own_ref.at[:, rows, :], out_sem.at[i])

    def join(sl, i, into):
        first, size = PIECES[i]

        def column(cb, carry):
            lanes = lanes_of(cb)
            for v in range(2):
                rows = pl.ds(first, size)
                into[v, rows, lanes] = inc[sl, core, v, rows, lanes] + part[sl, v, rows, lanes]
            return carry

        lax.fori_loop(0, CB, column, 0)

    def wait_pert(j, i):
        fields, rows = pl.ds(slots[j] * VARS, VARS), pl.ds(*PIECES[i])
        pltpu.make_async_copy(
            pert.at[:, fields, rows, :], pv.at[:, fields, rows, :], pert_sem.at[j, i]).wait()

    edges, inner = PIECES[:2], PIECES[2:]
    load_g.wait()
    for i in range(2):
        wait_pert(0, i)
        to_core[i].wait_recv()
    project(mine, edges)
    start_both(*halos(mine))
    to_core[2].start()
    to_chip[2].start()

    load_c.wait()

    @pl.when(jnp.logical_not(has_up))
    def _():
        ct[...] = jnp.zeros(ct.shape, jnp.int32)

    @pl.when(jnp.logical_not(has_down))
    def _():
        cn[...] = jnp.zeros(cn.shape, jnp.int32)

    wait_recv_both(c_up, c_down)

    def weights(cb, carry):
        lanes = lanes_of(cb)
        for i in range(CX + 2 * HALO):
            x = i - HALO
            source, row = (ct, 8 + x) if x < 0 else (cn, x - CX) if x >= CX else (cv, x)
            c = jnp.broadcast_to(source[pl.ds(row, 1), lanes], (8, LANES))
            for t in range(1, SWEEPS):
                coef[t - 1, cb, i] = jnp.where(c > t, KX, 0.0)
        return carry

    lax.fori_loop(0, CB, weights, 0)

    zero_outside(mine)
    zero_outside(theirs)
    wait_pert(0, 2)
    to_core[2].wait_recv()
    project(mine, inner)
    inner_sweeps(mine, (0, 1))

    for i in range(2):
        to_chip[i].wait_recv()
        onward[i].start()
    for i in range(2):
        wait_pert(1, i)
        onward[i].wait_recv()
    project(theirs, edges)
    start_both(*halos(theirs))

    inner_sweeps(mine, (1, 2))
    to_chip[2].wait_recv()
    onward[2].start()
    increments(mine, inner)
    to_partner(mine, 2).start()

    wait_pert(1, 2)
    onward[2].wait_recv()
    project(theirs, inner)
    inner_sweeps(theirs, (0, 2))
    increments(theirs, inner)
    to_partner(theirs, 2).start()

    wait_recv_both(*halos(mine))
    outer_sweeps(mine)
    to_partner(theirs, 2).wait_recv()
    join(theirs, 2, csum)
    to_owner(2).start()
    increments(mine, edges)
    for i in range(2):
        to_partner(mine, i).start()

    wait_recv_both(*halos(theirs))
    outer_sweeps(theirs)
    increments(theirs, edges)
    for i in range(2):
        to_partner(theirs, i).start()
    for i in range(2):
        to_partner(theirs, i).wait_recv()
        join(theirs, i, csum)
        to_owner(i).start()

    for i in range(3):
        to_partner(mine, i).wait_recv()
        join(mine, i, osum)
        out_copy(i).start()
    for i in range(3):
        to_owner(i).wait_recv()
        out_copy(i).wait()

    for i in range(3):
        to_core[i].wait_send()
        to_chip[i].wait_send()
        onward[i].wait_send()
        to_owner(i).wait_send()
        for sl in slots:
            to_partner(sl, i).wait_send()
    wait_send_both(c_up, c_down)
    for sl in slots:
        wait_send_both(*halos(sl))


def per_device(gradient, perturbations, counts):
    members = perturbations.shape[0] * lax.axis_size("mem")
    strips = lax.axis_size("strip")
    norm = 1.0 / math.sqrt(members * FIELDS)
    own = gradient.shape
    dma = pltpu.SemaphoreType.DMA
    f32 = jnp.float32
    a, b = pl.pallas_call(
        lambda *refs: kernel(norm, strips, *refs),
        name="covariance",
        out_shape=[jax.ShapeDtypeStruct(own, f32)] * 2,
        in_specs=[pl.BlockSpec(memory_space=pltpu.HBM)] * 3,
        out_specs=[pl.BlockSpec(memory_space=pltpu.HBM)] * 2,
        scratch_shapes=[
            pltpu.VMEM(perturbations.shape, jnp.bfloat16),
            pltpu.VMEM((4, *own), f32),
            pltpu.VMEM(counts.shape, jnp.int32),
            pltpu.VMEM((8, NY), jnp.int32),
            pltpu.VMEM((8, NY), jnp.int32),
            pltpu.VMEM((SLOTS, 2, CB, CX * PITCH, LANES), f32),
            pltpu.VMEM((SLOTS, 2, 2, CB, HALO, 8, LANES), f32),
            pltpu.VMEM((SLOTS, 2, 2, CB, HALO, 8, LANES), f32),
            pltpu.VMEM((SLOTS, 2, SWEEPS, 2, CB, 8, LANES), f32),
            pltpu.VMEM((SWEEPS - 1, CB, CX + 2 * HALO, 8, LANES), f32),
            pltpu.VMEM((SLOTS, 2, 2, CX, NY), f32),
            pltpu.VMEM((SLOTS, 2, CX, NY), f32),
            pltpu.VMEM((2, CX, NY), f32),
            pltpu.VMEM((2, CX, NY), f32),
            dma((2, 3)), dma((2,)),
            dma((3, 3)), dma((3, 3)),
            dma((2,)), dma((2,)),
            dma((2, 2)), dma((2, 2)),
            dma((2, 3)), dma((2, 3)),
            dma((3,)), dma((3,)), dma((3,)),
        ],
        compiler_params=pltpu.CompilerParams(
            collective_id=0, has_side_effects=True, vmem_limit_bytes=58000 * 1024),
    )(gradient, perturbations, counts)
    return a + b


def solution(mesh):
    return jax.shard_map(
        per_device,
        mesh=mesh,
        in_specs=(P("mem", "strip", None), P("mem", None, "strip", None), P("strip", None)),
        out_specs=P("mem", "strip", None),
        check_vma=False,
    )
```

```python
import math

import jax
import jax.numpy as jnp
from jax import lax
from jax.experimental import pallas as pl
from jax.experimental.pallas import tpu as pltpu
from jax.sharding import PartitionSpec as P

MESH = pl.DeviceIdType.MESH
SLOTS, VARS, FIELDS, SWEEPS = 2, 4, 8, 4
CX, NY, K = 32, 1024, 16
LANES = 128
CB = NY // LANES
HALO = SWEEPS
UNROLL = 2
TURN = 8
KX, KY = 0.35, 0.12
ALPHA = KY / KX
GAMMA = (1.0 - 2.0 * KX - 2.0 * KY) / KX
BETA = 2.0 + 2.0 * ALPHA
PITCH = 9
PIECES = ((0, 8), (24, 8), (8, 16))


def remote(src, dst, send, recv, device):
    return pltpu.make_async_remote_copy(
        src_ref=src, dst_ref=dst, send_sem=send, recv_sem=recv, device_id=device, device_id_type=MESH
    )


def lanes_of(cb):
    return pl.ds(pl.multiple_of(cb * LANES, LANES), LANES)


def kernel(
    norm, strips,
    grad, pert, counts, own_ref, other_ref,
    pv, gv, cv, ct, cn, u, near, sent, hop, edge, coef, inc, part, csum, osum,
    pert_sem, load_sem, gsend, grecv, csend, crecv, hsend, hrecv, jsend, jrecv, psend, precv, rsend, rrecv, out_sem,
):
    m, s = lax.axis_index("mem"), lax.axis_index("strip")
    chip, core = lax.div(m, 2), lax.rem(m, 2)
    m1, m2 = m + 1 - 2 * core, lax.rem(m + 2, 4)
    m3 = m2 + 1 - 2 * core
    mine, theirs = chip, 1 - chip
    has_up, has_down = s > 0, s < strips - 1
    slots = (mine, theirs)
    z = lax.rem(s, TURN)
    turn_up, turn_down = jnp.logical_and(has_up, z == 0), jnp.logical_and(has_down, z == TURN - 1)
    relay_down = jnp.logical_and(z == 1, s + TURN - 1 < strips)
    relay_up = jnp.logical_and(z == TURN - 2, s >= TURN - 1)
    roles = (
        (turn_up, s + TURN - 2, s - TURN + 1), (turn_down, s - TURN + 2, s + TURN - 1),
        (relay_down, s + TURN - 2, s + TURN - 1), (relay_up, s - TURN + 2, s - TURN + 1),
    )

    loads = []
    for i, (first, size) in enumerate(PIECES):
        for j, sl in enumerate(slots):
            fields, rows = pl.ds(sl * VARS, VARS), pl.ds(first, size)
            loads.append(pltpu.make_async_copy(
                pert.at[:, fields, rows, :], pv.at[:, fields, rows, :], pert_sem.at[j, i]))
    load_g = pltpu.make_async_copy(grad, gv.at[m], load_sem.at[0])
    load_c = pltpu.make_async_copy(counts, cv, load_sem.at[1])
    load_g.start()
    load_c.start()
    for copy in loads:
        copy.start()

    barrier = pltpu.get_barrier_semaphore()
    for device in ((m1, s), (m2, s)):
        pl.semaphore_signal(barrier, inc=1, device_id=device, device_id_type=MESH)

    @pl.when(has_up)
    def _():
        pl.semaphore_signal(barrier, inc=1, device_id=(m, s - 1), device_id_type=MESH)

    @pl.when(has_down)
    def _():
        pl.semaphore_signal(barrier, inc=1, device_id=(m, s + 1), device_id_type=MESH)

    expected = 2 + has_up.astype(jnp.int32) + has_down.astype(jnp.int32)
    for role, *others in roles:
        expected = expected + 2 * role.astype(jnp.int32)
        for other in others:
            @pl.when(role)
            def _(other=other):
                pl.semaphore_signal(barrier, inc=1, device_id=(m, other), device_id_type=MESH)

    pl.semaphore_wait(barrier, expected)

    to_core, to_chip, onward = [], [], []
    for i, (first, size) in enumerate(PIECES):
        rows = pl.ds(first, size)
        to_core.append(remote(grad.at[:, rows, :], gv.at[m, :, rows, :], gsend.at[0, i], grecv.at[0, i], (m1, s)))
        to_chip.append(remote(grad.at[:, rows, :], gv.at[m, :, rows, :], gsend.at[1, i], grecv.at[1, i], (m2, s)))
        onward.append(remote(
            gv.at[m2, :, rows, :], gv.at[m2, :, rows, :], gsend.at[2, i], grecv.at[2, i], (m1, s)))
    c_up = remote(counts.at[pl.ds(0, 8), :], cn, csend.at[0], crecv.at[0], (m, s - 1))
    c_down = remote(counts.at[pl.ds(24, 8), :], ct, csend.at[1], crecv.at[1], (m, s + 1))

    def halo(sl, side, h):
        device = (m, s - 1 if side == 0 else s + 1)
        return remote(sent.at[sl, side, h], near.at[sl, 1 - side, h], hsend.at[sl, side, h], hrecv.at[sl, side, h], device)

    def to_relay(sl, side):
        device = (m, s + TURN - 2 if side == 0 else s - TURN + 2)
        return remote(sent.at[sl, side, 1], hop.at[sl], hsend.at[sl, side, 1], jrecv.at[sl], device)

    def from_relay(sl, side):
        device = (m, s - TURN + 1 if side == 0 else s + TURN - 1)
        return remote(hop.at[sl], near.at[sl, 1 - side, 1], jsend.at[sl], hrecv.at[sl, side, 1], device)

    sides = ((0, has_up, turn_up, relay_up), (1, has_down, turn_down, relay_down))

    def send_halos(sl):
        for side, has, turn, _ in sides:
            @pl.when(has)
            def _():
                halo(sl, side, 0).start()

            @pl.when(jnp.logical_and(has, jnp.logical_not(turn)))
            def _():
                halo(sl, side, 1).start()

            @pl.when(turn)
            def _():
                to_relay(sl, side).start()

    def pass_on(sl):
        for side, _, _, relay in sides:
            @pl.when(relay)
            def _():
                to_relay(sl, side).wait_recv()
                from_relay(sl, side).start()

    def wait_halos(sl):
        for side, has in ((0, has_down), (1, has_up)):
            @pl.when(has)
            def _():
                for h in range(2):
                    halo(sl, side, h).wait_recv()

    def end_halos(sl):
        for side, has, _, relay in sides:
            @pl.when(has)
            def _():
                for h in range(2):
                    halo(sl, side, h).wait_send()

            @pl.when(relay)
            def _():
                from_relay(sl, side).wait_send()

    def start_both(up, down):
        @pl.when(has_up)
        def _():
            up.start()

        @pl.when(has_down)
        def _():
            down.start()

    def wait_recv_both(up, down):
        @pl.when(has_down)
        def _():
            up.wait_recv()

        @pl.when(has_up)
        def _():
            down.wait_recv()

    def wait_send_both(up, down):
        @pl.when(has_up)
        def _():
            up.wait_send()

        @pl.when(has_down)
        def _():
            down.wait_send()

    start_both(c_up, c_down)
    for i in range(2):
        to_chip[i].start()
        to_core[i].start()

    def project(sl, pieces):
        def column(cb, carry):
            lanes = lanes_of(cb)
            for first, size in pieces:
                rows = pl.ds(first, size)
                g = [gv[2 * sl + v // 2, v % 2, rows, lanes] for v in range(VARS)]
                for k in range(K):
                    total = pv[k, sl * VARS, rows, lanes].astype(jnp.float32) * g[0]
                    for v in range(1, VARS):
                        total = total + pv[k, sl * VARS + v, rows, lanes].astype(jnp.float32) * g[v]
                    for i in range(0, size, 8):
                        u[sl, k // 8, cb, pl.ds((first + i) * PITCH + k % 8, 8, stride=PITCH), :] = total[i : i + 8]
            for side, x0 in ((0, 0), (1, CX - HALO)):
                if any(first <= x0 < first + size for first, size in pieces):
                    for i in range(HALO):
                        for h in range(2):
                            sent[sl, side, h, cb, i] = u[sl, h, cb, pl.ds((x0 + i) * PITCH, 8), :]
            return carry

        lax.fori_loop(0, CB, column, 0, unroll=UNROLL)

    def zero_outside(sl):
        @pl.when(jnp.logical_not(has_up))
        def _():
            near[sl, 0] = jnp.zeros(near.shape[2:], jnp.float32)

        @pl.when(jnp.logical_not(has_down))
        def _():
            near[sl, 1] = jnp.zeros(near.shape[2:], jnp.float32)

    lane = lax.broadcasted_iota(jnp.int32, (8, LANES), 1)
    at_first, at_last = lane == 0, lane == LANES - 1
    zero = jnp.zeros((8, LANES), jnp.float32)
    on_grid = [jnp.where(has, jnp.ones((8, LANES), jnp.float32), 0.0) for has in (has_up, has_down)]

    def row_of(sl, x, h):
        if x < 0:
            return [near[sl, 0, h, cb, HALO + x] for cb in range(CB)]
        if x >= CX:
            return [near[sl, 1, h, cb, x - CX] for cb in range(CB)]
        return [u[sl, h, cb, pl.ds(x * PITCH, 8), :] for cb in range(CB)]

    def put_row(sl, x, h, values):
        for cb in range(CB):
            if x < 0:
                near[sl, 0, h, cb, HALO + x] = values[cb]
            elif x >= CX:
                near[sl, 1, h, cb, x - CX] = values[cb]
            else:
                u[sl, h, cb, pl.ds(x * PITCH, 8), :] = values[cb]

    def advanced(before, centre, after, t, x):
        right = [pltpu.roll(c, 1, 1) for c in centre]
        left = [pltpu.roll(c, LANES - 1, 1) for c in centre]
        out = []
        for cb in range(CB):
            low = jnp.where(at_first, right[cb - 1] if cb > 0 else zero, right[cb])
            high = jnp.where(at_last, left[cb + 1] if cb < CB - 1 else zero, left[cb])
            total = (before[cb] + after[cb]) + ALPHA * (low + high)
            if t == 0:
                total = total + GAMMA * centre[cb]
                out.append(total if 0 <= x < CX else on_grid[x >= CX] * total)
            else:
                out.append(centre[cb] + coef[t - 1, cb, HALO + x] * (total - BETA * centre[cb]))
        return out

    def inner_sweeps(sl, halves):
        def half(h, carry):
            for t in range(SWEEPS):
                first, last = t + 1, CX - 2 - t
                before, centre = row_of(sl, first - 1, h), row_of(sl, first, h)
                for cb in range(CB):
                    edge[sl, 0, t, h, cb] = centre[cb]
                for x in range(first, last + 1):
                    after = row_of(sl, x + 1, h)
                    if x == last:
                        for cb in range(CB):
                            edge[sl, 1, t, h, cb] = centre[cb]
                    put_row(sl, x, h, advanced(before, centre, after, t, x))
                    before, centre = centre, after
            return carry

        lax.fori_loop(*halves, half, 0)

    def outer_sweeps(sl):
        def half(h, carry):
            for t in range(SWEEPS):
                before, centre = row_of(sl, t - HALO, h), row_of(sl, t - HALO + 1, h)
                for x in range(t - HALO + 1, t + 1):
                    after = [edge[sl, 0, t, h, cb] for cb in range(CB)] if x == t else row_of(sl, x + 1, h)
                    put_row(sl, x, h, advanced(before, centre, after, t, x))
                    before, centre = centre, after
                before, centre = [edge[sl, 1, t, h, cb] for cb in range(CB)], row_of(sl, CX - 1 - t, h)
                for x in range(CX - 1 - t, CX + HALO - 1 - t):
                    after = row_of(sl, x + 1, h)
                    put_row(sl, x, h, advanced(before, centre, after, t, x))
                    before, centre = centre, after
            return carry

        lax.fori_loop(0, 2, half, 0)

    def increments(sl, pieces):
        def column(cb, carry):
            lanes = lanes_of(cb)
            for first, size in pieces:
                for x in range(first, first + size, 8):
                    rows = pl.ds(x, 8)
                    total = [None] * VARS
                    for k in range(K):
                        smooth = u[sl, k // 8, cb, pl.ds(x * PITCH + k % 8, 8, stride=PITCH), :]
                        for v in range(VARS):
                            term = pv[k, sl * VARS + v, rows, lanes].astype(jnp.float32) * smooth
                            total[v] = term if k == 0 else total[v] + term
                    for v in range(VARS):
                        inc[sl, v // 2, v % 2, rows, lanes] = total[v] * (norm * KX)
            return carry

        lax.fori_loop(0, CB, column, 0, unroll=UNROLL)

    def to_partner(sl, i):
        rows = pl.ds(*PIECES[i])
        return remote(inc.at[sl, 1 - core, :, rows, :], part.at[sl, :, rows, :],
                      psend.at[sl, i], precv.at[sl, i], (m1, s))

    def to_owner(i):
        rows = pl.ds(*PIECES[i])
        return remote(csum.at[:, rows, :], other_ref.at[:, rows, :], rsend.at[i], rrecv.at[i], (m2, s))

    def out_copy(i):
        rows = pl.ds(*PIECES[i])
        return pltpu.make_async_copy(osum.at[:, rows, :], own_ref.at[:, rows, :], out_sem.at[i])

    def join(sl, i, into):
        first, size = PIECES[i]

        def column(cb, carry):
            lanes = lanes_of(cb)
            for v in range(2):
                rows = pl.ds(first, size)
                into[v, rows, lanes] = inc[sl, core, v, rows, lanes] + part[sl, v, rows, lanes]
            return carry

        lax.fori_loop(0, CB, column, 0)

    def wait_pert(j, i):
        fields, rows = pl.ds(slots[j] * VARS, VARS), pl.ds(*PIECES[i])
        pltpu.make_async_copy(
            pert.at[:, fields, rows, :], pv.at[:, fields, rows, :], pert_sem.at[j, i]).wait()

    edges, inner = PIECES[:2], PIECES[2:]
    load_g.wait()
    for i in range(2):
        wait_pert(0, i)
        to_core[i].wait_recv()
    project(mine, edges)
    send_halos(mine)
    to_core[2].start()
    to_chip[2].start()

    load_c.wait()

    def weights(rows):
        def column(cb, carry):
            lanes = lanes_of(cb)
            for x in rows:
                source, row = (ct, 8 + x) if x < 0 else (cn, x - CX) if x >= CX else (cv, x)
                c = jnp.broadcast_to(source[pl.ds(row, 1), lanes], (8, LANES))
                for t in range(1, SWEEPS):
                    coef[t - 1, cb, HALO + x] = jnp.where(c > t, KX, 0.0)
            return carry

        lax.fori_loop(0, CB, column, 0)

    weights(range(CX))
    wait_pert(0, 2)
    to_core[2].wait_recv()
    project(mine, inner)
    inner_sweeps(mine, (0, 1))

    for i in range(2):
        to_chip[i].wait_recv()
        onward[i].start()
    for i in range(2):
        wait_pert(1, i)
        onward[i].wait_recv()
    project(theirs, edges)
    send_halos(theirs)
    pass_on(mine)

    inner_sweeps(mine, (1, 2))
    to_chip[2].wait_recv()
    onward[2].start()
    wait_pert(1, 2)
    onward[2].wait_recv()
    project(theirs, inner)
    inner_sweeps(theirs, (0, 1))
    pass_on(theirs)
    inner_sweeps(theirs, (1, 2))
    increments(theirs, inner)
    to_partner(theirs, 2).start()
    increments(mine, inner)
    to_partner(mine, 2).start()
    to_partner(theirs, 2).wait_recv()
    join(theirs, 2, csum)
    to_owner(2).start()

    zero_outside(mine)
    zero_outside(theirs)

    @pl.when(jnp.logical_not(has_up))
    def _():
        ct[...] = jnp.zeros(ct.shape, jnp.int32)

    @pl.when(jnp.logical_not(has_down))
    def _():
        cn[...] = jnp.zeros(cn.shape, jnp.int32)

    wait_recv_both(c_up, c_down)
    weights([*range(-HALO, 0), *range(CX, CX + HALO)])
    wait_halos(mine)
    outer_sweeps(mine)
    increments(mine, edges)
    for i in range(2):
        to_partner(mine, i).start()

    wait_halos(theirs)
    outer_sweeps(theirs)
    increments(theirs, edges)
    for i in range(2):
        to_partner(theirs, i).start()
    for i in range(2):
        to_partner(theirs, i).wait_recv()
        join(theirs, i, csum)
        to_owner(i).start()

    for i in range(3):
        to_partner(mine, i).wait_recv()
        join(mine, i, osum)
        out_copy(i).start()
    for i in range(3):
        to_owner(i).wait_recv()
        out_copy(i).wait()

    for i in range(3):
        to_core[i].wait_send()
        to_chip[i].wait_send()
        onward[i].wait_send()
        to_owner(i).wait_send()
        for sl in slots:
            to_partner(sl, i).wait_send()
    wait_send_both(c_up, c_down)
    for sl in slots:
        end_halos(sl)


def per_device(gradient, perturbations, counts):
    members = perturbations.shape[0] * lax.axis_size("mem")
    strips = lax.axis_size("strip")
    norm = 1.0 / math.sqrt(members * FIELDS)
    own = gradient.shape
    dma = pltpu.SemaphoreType.DMA
    f32 = jnp.float32
    a, b = pl.pallas_call(
        lambda *refs: kernel(norm, strips, *refs),
        name="covariance",
        out_shape=[jax.ShapeDtypeStruct(own, f32)] * 2,
        in_specs=[pl.BlockSpec(memory_space=pltpu.HBM)] * 3,
        out_specs=[pl.BlockSpec(memory_space=pltpu.HBM)] * 2,
        scratch_shapes=[
            pltpu.VMEM(perturbations.shape, jnp.bfloat16),
            pltpu.VMEM((4, *own), f32),
            pltpu.VMEM(counts.shape, jnp.int32),
            pltpu.VMEM((8, NY), jnp.int32),
            pltpu.VMEM((8, NY), jnp.int32),
            pltpu.VMEM((SLOTS, 2, CB, CX * PITCH, LANES), f32),
            pltpu.VMEM((SLOTS, 2, 2, CB, HALO, 8, LANES), f32),
            pltpu.VMEM((SLOTS, 2, 2, CB, HALO, 8, LANES), f32),
            pltpu.VMEM((SLOTS, CB, HALO, 8, LANES), f32),
            pltpu.VMEM((SLOTS, 2, SWEEPS, 2, CB, 8, LANES), f32),
            pltpu.VMEM((SWEEPS - 1, CB, CX + 2 * HALO, 8, LANES), f32),
            pltpu.VMEM((SLOTS, 2, 2, CX, NY), f32),
            pltpu.VMEM((SLOTS, 2, CX, NY), f32),
            pltpu.VMEM((2, CX, NY), f32),
            pltpu.VMEM((2, CX, NY), f32),
            dma((2, 3)), dma((2,)),
            dma((3, 3)), dma((3, 3)),
            dma((2,)), dma((2,)),
            dma((2, 2, 2)), dma((2, 2, 2)), dma((2,)), dma((2,)),
            dma((2, 3)), dma((2, 3)),
            dma((3,)), dma((3,)), dma((3,)),
        ],
        compiler_params=pltpu.CompilerParams(
            collective_id=0, has_side_effects=True, vmem_limit_bytes=58000 * 1024),
    )(gradient, perturbations, counts)
    return a + b


def solution(mesh):
    return jax.shard_map(
        per_device,
        mesh=mesh,
        in_specs=(P("mem", "strip", None), P("mem", None, "strip", None), P("strip", None)),
        out_specs=P("mem", "strip", None),
        check_vma=False,
    )
```

```python
import math

import jax
import jax.numpy as jnp
from jax import lax
from jax.experimental import pallas as pl
from jax.experimental.pallas import tpu as pltpu
from jax.sharding import PartitionSpec as P

MESH = pl.DeviceIdType.MESH
SLOTS, VARS, FIELDS, SWEEPS = 2, 4, 8, 4
CX, NY, K = 32, 1024, 16
LANES = 128
CB = NY // LANES
HALO = SWEEPS
UNROLL = 2
TURN = 8
KX, KY = 0.35, 0.12
ALPHA = KY / KX
GAMMA = (1.0 - 2.0 * KX - 2.0 * KY) / KX
BETA = 2.0 + 2.0 * ALPHA
PITCH = 9
PIECES = ((0, 8), (24, 8), (8, 16))


def remote(src, dst, send, recv, device):
    return pltpu.make_async_remote_copy(
        src_ref=src, dst_ref=dst, send_sem=send, recv_sem=recv, device_id=device, device_id_type=MESH
    )


def lanes_of(cb):
    return pl.ds(pl.multiple_of(cb * LANES, LANES), LANES)


def kernel(
    norm, strips,
    grad, pert, counts, own_ref, other_ref,
    pv, gv, cv, ct, cn, u, near, sent, hop, edge, coef, inc, part, csum, osum,
    pert_sem, load_sem, gsend, grecv, csend, crecv, hsend, hrecv, jsend, jrecv, psend, precv, rsend, rrecv, out_sem,
):
    m, s = lax.axis_index("mem"), lax.axis_index("strip")
    chip, core = lax.div(m, 2), lax.rem(m, 2)
    m1, m2 = m + 1 - 2 * core, lax.rem(m + 2, 4)
    m3 = m2 + 1 - 2 * core
    mine, theirs = chip, 1 - chip
    has_up, has_down = s > 0, s < strips - 1
    slots = (mine, theirs)
    z = lax.rem(s, TURN)
    turn_up, turn_down = jnp.logical_and(has_up, z == 0), jnp.logical_and(has_down, z == TURN - 1)
    relay_down = jnp.logical_and(z == 1, s + TURN - 1 < strips)
    relay_up = jnp.logical_and(z == TURN - 2, s >= TURN - 1)
    roles = (
        (turn_up, s + TURN - 2, s - TURN + 1), (turn_down, s - TURN + 2, s + TURN - 1),
        (relay_down, s + TURN - 2, s + TURN - 1), (relay_up, s - TURN + 2, s - TURN + 1),
    )

    loads = []
    for i, (first, size) in enumerate(PIECES):
        for j, sl in enumerate(slots):
            fields, rows = pl.ds(sl * VARS, VARS), pl.ds(first, size)
            loads.append(pltpu.make_async_copy(
                pert.at[:, fields, rows, :], pv.at[:, fields, rows, :], pert_sem.at[j, i]))
    load_g = pltpu.make_async_copy(grad, gv.at[m], load_sem.at[0])
    load_c = pltpu.make_async_copy(counts, cv, load_sem.at[1])
    load_g.start()
    load_c.start()
    for copy in loads:
        copy.start()

    barrier = pltpu.get_barrier_semaphore()
    for device in ((m1, s), (m2, s)):
        pl.semaphore_signal(barrier, inc=1, device_id=device, device_id_type=MESH)

    @pl.when(has_up)
    def _():
        pl.semaphore_signal(barrier, inc=1, device_id=(m, s - 1), device_id_type=MESH)

    @pl.when(has_down)
    def _():
        pl.semaphore_signal(barrier, inc=1, device_id=(m, s + 1), device_id_type=MESH)

    expected = 2 + has_up.astype(jnp.int32) + has_down.astype(jnp.int32)
    for role, *others in roles:
        expected = expected + 2 * role.astype(jnp.int32)
        for other in others:
            @pl.when(role)
            def _(other=other):
                pl.semaphore_signal(barrier, inc=1, device_id=(m, other), device_id_type=MESH)

    pl.semaphore_wait(barrier, expected)

    to_core, to_chip, onward = [], [], []
    for i, (first, size) in enumerate(PIECES):
        rows = pl.ds(first, size)
        to_core.append(remote(grad.at[:, rows, :], gv.at[m, :, rows, :], gsend.at[0, i], grecv.at[0, i], (m1, s)))
        to_chip.append(remote(grad.at[:, rows, :], gv.at[m, :, rows, :], gsend.at[1, i], grecv.at[1, i], (m2, s)))
        onward.append(remote(
            gv.at[m2, :, rows, :], gv.at[m2, :, rows, :], gsend.at[2, i], grecv.at[2, i], (m1, s)))
    c_up = remote(counts.at[pl.ds(0, 8), :], cn, csend.at[0], crecv.at[0], (m, s - 1))
    c_down = remote(counts.at[pl.ds(24, 8), :], ct, csend.at[1], crecv.at[1], (m, s + 1))

    def halo(sl, side, h):
        device = (m, s - 1 if side == 0 else s + 1)
        return remote(sent.at[sl, side, h], near.at[sl, 1 - side, h], hsend.at[sl, side, h], hrecv.at[sl, side, h], device)

    def to_relay(sl, side):
        device = (m, s + TURN - 2 if side == 0 else s - TURN + 2)
        return remote(sent.at[sl, side, 1], hop.at[sl], hsend.at[sl, side, 1], jrecv.at[sl], device)

    def from_relay(sl, side):
        device = (m, s - TURN + 1 if side == 0 else s + TURN - 1)
        return remote(hop.at[sl], near.at[sl, 1 - side, 1], jsend.at[sl], hrecv.at[sl, side, 1], device)

    sides = ((0, has_up, turn_up, relay_up), (1, has_down, turn_down, relay_down))

    def send_halos(sl):
        for side, has, turn, _ in sides:
            @pl.when(turn)
            def _():
                to_relay(sl, side).start()

            @pl.when(has)
            def _():
                halo(sl, side, 0).start()

            @pl.when(jnp.logical_and(has, jnp.logical_not(turn)))
            def _():
                halo(sl, side, 1).start()

    def pass_on(sl):
        for side, _, _, relay in sides:
            @pl.when(relay)
            def _():
                to_relay(sl, side).wait_recv()
                from_relay(sl, side).start()

    def wait_halos(sl):
        for side, has in ((0, has_down), (1, has_up)):
            @pl.when(has)
            def _():
                for h in range(2):
                    halo(sl, side, h).wait_recv()

    def end_halos(sl):
        for side, has, _, relay in sides:
            @pl.when(has)
            def _():
                for h in range(2):
                    halo(sl, side, h).wait_send()

            @pl.when(relay)
            def _():
                from_relay(sl, side).wait_send()

    def start_both(up, down):
        @pl.when(has_up)
        def _():
            up.start()

        @pl.when(has_down)
        def _():
            down.start()

    def wait_recv_both(up, down):
        @pl.when(has_down)
        def _():
            up.wait_recv()

        @pl.when(has_up)
        def _():
            down.wait_recv()

    def wait_send_both(up, down):
        @pl.when(has_up)
        def _():
            up.wait_send()

        @pl.when(has_down)
        def _():
            down.wait_send()

    start_both(c_up, c_down)
    for i in range(2):
        to_chip[i].start()
        to_core[i].start()

    def project(sl, pieces):
        def column(cb, carry):
            lanes = lanes_of(cb)
            for first, size in pieces:
                rows = pl.ds(first, size)
                g = [gv[2 * sl + v // 2, v % 2, rows, lanes] for v in range(VARS)]
                for k in range(K):
                    total = pv[k, sl * VARS, rows, lanes].astype(jnp.float32) * g[0]
                    for v in range(1, VARS):
                        total = total + pv[k, sl * VARS + v, rows, lanes].astype(jnp.float32) * g[v]
                    for i in range(0, size, 8):
                        u[sl, k // 8, cb, pl.ds((first + i) * PITCH + k % 8, 8, stride=PITCH), :] = total[i : i + 8]
            for side, x0 in ((0, 0), (1, CX - HALO)):
                if any(first <= x0 < first + size for first, size in pieces):
                    for i in range(HALO):
                        for h in range(2):
                            sent[sl, side, h, cb, i] = u[sl, h, cb, pl.ds((x0 + i) * PITCH, 8), :]
            return carry

        lax.fori_loop(0, CB, column, 0, unroll=UNROLL)

    def zero_outside(sl):
        @pl.when(jnp.logical_not(has_up))
        def _():
            near[sl, 0] = jnp.zeros(near.shape[2:], jnp.float32)

        @pl.when(jnp.logical_not(has_down))
        def _():
            near[sl, 1] = jnp.zeros(near.shape[2:], jnp.float32)

    lane = lax.broadcasted_iota(jnp.int32, (8, LANES), 1)
    at_first, at_last = lane == 0, lane == LANES - 1
    zero = jnp.zeros((8, LANES), jnp.float32)
    on_grid = [jnp.where(has, jnp.ones((8, LANES), jnp.float32), 0.0) for has in (has_up, has_down)]

    def row_of(sl, x, h):
        if x < 0:
            return [near[sl, 0, h, cb, HALO + x] for cb in range(CB)]
        if x >= CX:
            return [near[sl, 1, h, cb, x - CX] for cb in range(CB)]
        return [u[sl, h, cb, pl.ds(x * PITCH, 8), :] for cb in range(CB)]

    def put_row(sl, x, h, values):
        for cb in range(CB):
            if x < 0:
                near[sl, 0, h, cb, HALO + x] = values[cb]
            elif x >= CX:
                near[sl, 1, h, cb, x - CX] = values[cb]
            else:
                u[sl, h, cb, pl.ds(x * PITCH, 8), :] = values[cb]

    def advanced(before, centre, after, t, x):
        right = [pltpu.roll(c, 1, 1) for c in centre]
        left = [pltpu.roll(c, LANES - 1, 1) for c in centre]
        out = []
        for cb in range(CB):
            low = jnp.where(at_first, right[cb - 1] if cb > 0 else zero, right[cb])
            high = jnp.where(at_last, left[cb + 1] if cb < CB - 1 else zero, left[cb])
            total = (before[cb] + after[cb]) + ALPHA * (low + high)
            if t == 0:
                total = total + GAMMA * centre[cb]
                out.append(total if 0 <= x < CX else on_grid[x >= CX] * total)
            else:
                out.append(centre[cb] + coef[t - 1, cb, HALO + x] * (total - BETA * centre[cb]))
        return out

    def inner_sweeps(sl, halves):
        def half(h, carry):
            for t in range(SWEEPS):
                first, last = t + 1, CX - 2 - t
                before, centre = row_of(sl, first - 1, h), row_of(sl, first, h)
                for cb in range(CB):
                    edge[sl, 0, t, h, cb] = centre[cb]
                for x in range(first, last + 1):
                    after = row_of(sl, x + 1, h)
                    if x == last:
                        for cb in range(CB):
                            edge[sl, 1, t, h, cb] = centre[cb]
                    put_row(sl, x, h, advanced(before, centre, after, t, x))
                    before, centre = centre, after
            return carry

        lax.fori_loop(*halves, half, 0)

    def outer_sweeps(sl):
        def half(h, carry):
            for t in range(SWEEPS):
                before, centre = row_of(sl, t - HALO, h), row_of(sl, t - HALO + 1, h)
                for x in range(t - HALO + 1, t + 1):
                    after = [edge[sl, 0, t, h, cb] for cb in range(CB)] if x == t else row_of(sl, x + 1, h)
                    put_row(sl, x, h, advanced(before, centre, after, t, x))
                    before, centre = centre, after
                before, centre = [edge[sl, 1, t, h, cb] for cb in range(CB)], row_of(sl, CX - 1 - t, h)
                for x in range(CX - 1 - t, CX + HALO - 1 - t):
                    after = row_of(sl, x + 1, h)
                    put_row(sl, x, h, advanced(before, centre, after, t, x))
                    before, centre = centre, after
            return carry

        lax.fori_loop(0, 2, half, 0)

    def increments(sl, pieces):
        def column(cb, carry):
            lanes = lanes_of(cb)
            for first, size in pieces:
                for x in range(first, first + size, 8):
                    rows = pl.ds(x, 8)
                    total = [None] * VARS
                    for k in range(K):
                        smooth = u[sl, k // 8, cb, pl.ds(x * PITCH + k % 8, 8, stride=PITCH), :]
                        for v in range(VARS):
                            term = pv[k, sl * VARS + v, rows, lanes].astype(jnp.float32) * smooth
                            total[v] = term if k == 0 else total[v] + term
                    for v in range(VARS):
                        inc[sl, v // 2, v % 2, rows, lanes] = total[v] * (norm * KX)
            return carry

        lax.fori_loop(0, CB, column, 0, unroll=UNROLL)

    def to_partner(sl, i):
        rows = pl.ds(*PIECES[i])
        return remote(inc.at[sl, 1 - core, :, rows, :], part.at[sl, :, rows, :],
                      psend.at[sl, i], precv.at[sl, i], (m1, s))

    def to_owner(i):
        rows = pl.ds(*PIECES[i])
        return remote(csum.at[:, rows, :], other_ref.at[:, rows, :], rsend.at[i], rrecv.at[i], (m2, s))

    def out_copy(i):
        rows = pl.ds(*PIECES[i])
        return pltpu.make_async_copy(osum.at[:, rows, :], own_ref.at[:, rows, :], out_sem.at[i])

    def join(sl, i, into):
        first, size = PIECES[i]

        def column(cb, carry):
            lanes = lanes_of(cb)
            for v in range(2):
                rows = pl.ds(first, size)
                into[v, rows, lanes] = inc[sl, core, v, rows, lanes] + part[sl, v, rows, lanes]
            return carry

        lax.fori_loop(0, CB, column, 0)

    def wait_pert(j, i):
        fields, rows = pl.ds(slots[j] * VARS, VARS), pl.ds(*PIECES[i])
        pltpu.make_async_copy(
            pert.at[:, fields, rows, :], pv.at[:, fields, rows, :], pert_sem.at[j, i]).wait()

    edges, inner = PIECES[:2], PIECES[2:]
    load_g.wait()
    for i in range(2):
        wait_pert(0, i)
        to_core[i].wait_recv()
    project(mine, edges)
    send_halos(mine)
    to_core[2].start()
    to_chip[2].start()

    load_c.wait()

    def weights(rows):
        def column(cb, carry):
            lanes = lanes_of(cb)
            for x in rows:
                source, row = (ct, 8 + x) if x < 0 else (cn, x - CX) if x >= CX else (cv, x)
                c = jnp.broadcast_to(source[pl.ds(row, 1), lanes], (8, LANES))
                for t in range(1, SWEEPS):
                    coef[t - 1, cb, HALO + x] = jnp.where(c > t, KX, 0.0)
            return carry

        lax.fori_loop(0, CB, column, 0)

    weights(range(CX))
    wait_pert(0, 2)
    to_core[2].wait_recv()
    project(mine, inner)
    inner_sweeps(mine, (0, 1))

    for i in range(2):
        to_chip[i].wait_recv()
        onward[i].start()
    for i in range(2):
        wait_pert(1, i)
        onward[i].wait_recv()
    project(theirs, edges)
    send_halos(theirs)
    pass_on(mine)

    inner_sweeps(mine, (1, 2))
    to_chip[2].wait_recv()
    onward[2].start()
    wait_pert(1, 2)
    onward[2].wait_recv()
    project(theirs, inner)
    inner_sweeps(theirs, (0, 1))
    pass_on(theirs)
    inner_sweeps(theirs, (1, 2))
    increments(theirs, inner)
    to_partner(theirs, 2).start()
    increments(mine, inner)
    to_partner(mine, 2).start()
    to_partner(theirs, 2).wait_recv()
    join(theirs, 2, csum)
    to_owner(2).start()

    zero_outside(mine)
    zero_outside(theirs)

    @pl.when(jnp.logical_not(has_up))
    def _():
        ct[...] = jnp.zeros(ct.shape, jnp.int32)

    @pl.when(jnp.logical_not(has_down))
    def _():
        cn[...] = jnp.zeros(cn.shape, jnp.int32)

    wait_recv_both(c_up, c_down)
    weights([*range(-HALO, 0), *range(CX, CX + HALO)])
    wait_halos(mine)
    outer_sweeps(mine)
    increments(mine, edges)
    for i in range(2):
        to_partner(mine, i).start()

    wait_halos(theirs)
    outer_sweeps(theirs)
    increments(theirs, edges)
    for i in range(2):
        to_partner(theirs, i).start()
    for i in range(2):
        to_partner(theirs, i).wait_recv()
        join(theirs, i, csum)
        to_owner(i).start()

    for i in range(3):
        to_partner(mine, i).wait_recv()
        join(mine, i, osum)
        out_copy(i).start()
    for i in range(3):
        to_owner(i).wait_recv()
        out_copy(i).wait()

    for i in range(3):
        to_core[i].wait_send()
        to_chip[i].wait_send()
        onward[i].wait_send()
        to_owner(i).wait_send()
        for sl in slots:
            to_partner(sl, i).wait_send()
    wait_send_both(c_up, c_down)
    for sl in slots:
        end_halos(sl)


def per_device(gradient, perturbations, counts):
    members = perturbations.shape[0] * lax.axis_size("mem")
    strips = lax.axis_size("strip")
    norm = 1.0 / math.sqrt(members * FIELDS)
    own = gradient.shape
    dma = pltpu.SemaphoreType.DMA
    f32 = jnp.float32
    a, b = pl.pallas_call(
        lambda *refs: kernel(norm, strips, *refs),
        name="covariance",
        out_shape=[jax.ShapeDtypeStruct(own, f32)] * 2,
        in_specs=[pl.BlockSpec(memory_space=pltpu.HBM)] * 3,
        out_specs=[pl.BlockSpec(memory_space=pltpu.HBM)] * 2,
        scratch_shapes=[
            pltpu.VMEM(perturbations.shape, jnp.bfloat16),
            pltpu.VMEM((4, *own), f32),
            pltpu.VMEM(counts.shape, jnp.int32),
            pltpu.VMEM((8, NY), jnp.int32),
            pltpu.VMEM((8, NY), jnp.int32),
            pltpu.VMEM((SLOTS, 2, CB, CX * PITCH, LANES), f32),
            pltpu.VMEM((SLOTS, 2, 2, CB, HALO, 8, LANES), f32),
            pltpu.VMEM((SLOTS, 2, 2, CB, HALO, 8, LANES), f32),
            pltpu.VMEM((SLOTS, CB, HALO, 8, LANES), f32),
            pltpu.VMEM((SLOTS, 2, SWEEPS, 2, CB, 8, LANES), f32),
            pltpu.VMEM((SWEEPS - 1, CB, CX + 2 * HALO, 8, LANES), f32),
            pltpu.VMEM((SLOTS, 2, 2, CX, NY), f32),
            pltpu.VMEM((SLOTS, 2, CX, NY), f32),
            pltpu.VMEM((2, CX, NY), f32),
            pltpu.VMEM((2, CX, NY), f32),
            dma((2, 3)), dma((2,)),
            dma((3, 3)), dma((3, 3)),
            dma((2,)), dma((2,)),
            dma((2, 2, 2)), dma((2, 2, 2)), dma((2,)), dma((2,)),
            dma((2, 3)), dma((2, 3)),
            dma((3,)), dma((3,)), dma((3,)),
        ],
        compiler_params=pltpu.CompilerParams(
            collective_id=0, has_side_effects=True, vmem_limit_bytes=58000 * 1024),
    )(gradient, perturbations, counts)
    return a + b


def solution(mesh):
    return jax.shard_map(
        per_device,
        mesh=mesh,
        in_specs=(P("mem", "strip", None), P("mem", None, "strip", None), P("strip", None)),
        out_specs=P("mem", "strip", None),
        check_vma=False,
    )
```
